768 devices in a mesh: outer: 24 (over x_hi, z), inner: 16 (over y, core), head: 2 (over x_lo).
Axes of the slice: x: 4 (x_hi: 2, x_lo: 2; x = x_hi * 2 + x_lo), y: 8, z: 12, core: 2. Of those that a mesh axis runs over, the one named last changes fastest.
Arguments:
- queries: bfloat16 [49152, 8, 1024], P(('outer', 'inner'), 'head'), may hold values from -7 to 7
- keys: bfloat16 [49152, 1024], P(('outer', 'inner')), may hold values from -4 to 4
- values: bfloat16 [49152, 1024], P(('outer', 'inner')), may hold values from -6 to 6
- grad_out: bfloat16 [49152, 8, 1024], P(('outer', 'inner'), 'head'), may hold values from -6 to 6
- positions: int32 [49152], P(('outer', 'inner')), may hold values from 0 to 18431, as said below
Outputs:
- grad_queries: bfloat16 [49152, 8, 1024], P(('outer', 'inner'), 'head')
- grad_keys: bfloat16 [49152, 1024], P(('outer', 'inner'), 'head')
- grad_values: bfloat16 [49152, 1024], P(('outer', 'inner'), 'head')
The draws below stay inside these ranges and needn't reach their ends.
Inputs may be any that keep to these rules, and one draw needn't show every extreme that they name: `positions`: time ids never fall along the sequence; every id is held by 2 to 4 consecutive tokens.
All inputs are finite; a program needn't handle non-finite values.
Results may differ from the reference program's by a relative error of at most 0.0055.
The reference program's roundings to bfloat16 on the way count: a program that leaves them out, or rounds other values in their place, can miss the bound.
Values may be sent and summed in bfloat16 or wider, within the bound.
A program may use at most 64 MiB of HBM per device.

```python
import math
import jax
import jax.numpy as jnp
import numpy as np
from jax import lax

HEAD = 128
KV_HEADS = 8
GROUP = 8
TOK_DEV = 128
WINDOW = 512
TOKENS = 49152


def time_ids(seed_key):
    row_ids = jnp.arange(TOKENS, dtype=jnp.int32)
    block_ids = row_ids // 8
    within = row_ids % 8
    pattern = jax.random.randint(seed_key, (TOKENS // 8,), 0, 6)
    first_ends = jnp.array([2, 2, 4, 2, 3, 3], jnp.int32)
    second_ends = jnp.array([4, 6, 6, 5, 5, 6], jnp.int32)
    chosen = pattern[block_ids]
    first_end = first_ends[chosen]
    second_end = second_ends[chosen]
    bumps = (within >= first_end).astype(jnp.int32) + (within >= second_end).astype(jnp.int32)
    return (3 * block_ids + bumps).astype(jnp.int32)


def key_entries(seed_key):
    width = KV_HEADS * HEAD
    entries = jnp.clip(jax.random.normal(jax.random.fold_in(seed_key, 11), (TOKENS, width), jnp.float32), -4.0, 4.0)
    return entries


def draw_positions(key, part):
    return time_ids(jax.random.fold_in(key, 7))


def draw_keys(key, part):
    entries = key_entries(key)
    return entries.astype(jnp.bfloat16)


def draw_queries(key, part):
    dims = (TOKENS, GROUP, KV_HEADS * HEAD)
    entries = jnp.clip(jax.random.normal(jax.random.fold_in(key, 12), dims, jnp.float32), -4.0, 4.0)
    return entries.astype(jnp.bfloat16)


def levels(stream_key, extent, pieces, low, largest):
    factor_of = 1.0
    for axis_at, shards_of in pieces:
        heights = jax.random.uniform(jax.random.fold_in(jax.random.fold_in(stream_key, 6), axis_at), (shards_of,), jnp.float32, low / len(pieces), largest / len(pieces))
        factor_of = factor_of * jnp.repeat(jnp.exp(heights), extent[axis_at] // shards_of).reshape((-1,) + (1,) * (len(extent) - 1 - axis_at))
    return factor_of


def gaussian(stream_key, shape, scale, reach, pieces=(), held_as=jnp.bfloat16):
    factor_of = levels(stream_key, shape, pieces, -0.22, 0.18) if pieces else 1.0
    values = jax.random.normal(stream_key, shape, jnp.float32) * scale * factor_of
    return jnp.minimum(jnp.maximum(values, -reach), reach).astype(held_as)


def setup_inputs(seed: int = 0) -> dict:
    key_list = jax.random.split(jax.random.key(seed), 6)
    queries = draw_queries(jax.random.fold_in(key_list[5], 71), 0)
    keys = draw_keys(jax.random.fold_in(key_list[5], 71), 0)
    values = gaussian(key_list[2], (TOKENS, KV_HEADS * HEAD), 1.0, 6.0, ((0, 384),))
    grad_out = gaussian(key_list[3], (TOKENS, GROUP, KV_HEADS * HEAD), 1.0, 6.0, ((0, 384), (1, 2)))
    positions = draw_positions(jax.random.fold_in(key_list[5], 71), 0)
    return {"queries": queries, "keys": keys, "values": values, "grad_out": grad_out, "positions": positions}


rope_theta = 500000.0
rope_factor = 128.0
initial_context = 8192.0
ramp_low = 1.0
ramp_high = 32.0
attention_factor = 1.0 + 0.1 * math.log(rope_factor)

def yarn_frequencies():
    halves = HEAD // 2
    powers = rope_theta ** (-2.0 * np.arange(halves) / HEAD)
    turns = initial_context * powers / (2.0 * np.pi)
    blend = np.clip((turns - ramp_low) / (ramp_high - ramp_low), 0.0, 1.0)
    return jnp.asarray(powers * ((1.0 - blend) / rope_factor + blend), jnp.float32)

def rope_tables(positions):
    frequency = yarn_frequencies()
    angles = positions.astype(jnp.float32)[:, None] * frequency[None, :]
    return (attention_factor * jnp.cos(angles), attention_factor * jnp.sin(angles))

def rotate(vector, cosines, sines):
    middle = vector.shape[-1] // 2
    leading = vector[..., :middle]
    trailing = vector[..., middle:]
    return jnp.concatenate([leading * cosines - trailing * sines, trailing * cosines + leading * sines], -1)

def unrotate(vector, cosines, sines):
    middle = vector.shape[-1] // 2
    leading = vector[..., :middle]
    trailing = vector[..., middle:]
    return jnp.concatenate([leading * cosines + trailing * sines, trailing * cosines - leading * sines], -1)

def reference(queries, keys, values, grad_out, positions):
    score_scale = 1.0 / math.sqrt(HEAD)
    cosines, sines = rope_tables(positions)
    rotated_keys = rotate(keys.reshape(TOKENS, KV_HEADS, HEAD).astype(jnp.float32), cosines[:, None, :], sines[:, None, :]).astype(jnp.bfloat16)
    padding = jnp.zeros((WINDOW, KV_HEADS, HEAD), jnp.bfloat16)
    keys_padded = jnp.concatenate([padding, rotated_keys], 0)
    values_padded = jnp.concatenate([padding, values.reshape(TOKENS, KV_HEADS, HEAD)], 0)
    window_len = WINDOW + TOK_DEV
    query_ids = jnp.arange(TOK_DEV, dtype=jnp.int32)[:, None]
    window_ids = jnp.arange(window_len, dtype=jnp.int32)[None, :]

    def one_block(carry, block_id):
        key_grads, value_grads = carry
        offset = (block_id * TOK_DEV).astype(jnp.int32)
        query_block = lax.dynamic_slice_in_dim(queries, offset, TOK_DEV, 0).reshape(TOK_DEV, GROUP, KV_HEADS, HEAD)
        grad_block = lax.dynamic_slice_in_dim(grad_out, offset, TOK_DEV, 0).reshape(TOK_DEV, GROUP, KV_HEADS, HEAD)
        block_cosines = lax.dynamic_slice_in_dim(cosines, offset, TOK_DEV, 0)[:, None, None, :]
        block_sines = lax.dynamic_slice_in_dim(sines, offset, TOK_DEV, 0)[:, None, None, :]
        rotated_queries = rotate(query_block.astype(jnp.float32), block_cosines, block_sines).astype(jnp.bfloat16)
        window_keys = lax.dynamic_slice_in_dim(keys_padded, offset, window_len, 0)
        window_values = lax.dynamic_slice_in_dim(values_padded, offset, window_len, 0)
        allowed = (window_ids > query_ids) & (window_ids <= query_ids + WINDOW) & (offset - WINDOW + window_ids >= 0)
        scores = jnp.einsum('aghd,whd->hgaw', rotated_queries.astype(jnp.float32), window_keys.astype(jnp.float32)) * score_scale
        scores = jnp.where(allowed, scores, -jnp.inf)
        row_max = lax.optimization_barrier(jnp.max(scores, -1, keepdims=True))
        raised = jnp.exp(scores - row_max)
        weights = raised / lax.optimization_barrier(jnp.sum(raised, -1, keepdims=True))
        weights_low = weights.astype(jnp.bfloat16)
        weight_grads = jnp.einsum('aghd,whd->hgaw', grad_block.astype(jnp.float32), window_values.astype(jnp.float32))
        row_terms = lax.optimization_barrier(jnp.sum(weights * weight_grads, -1, keepdims=True))
        score_grads = (weights * (weight_grads - row_terms)).astype(jnp.bfloat16)
        query_grads = jnp.einsum('hgaw,whd->aghd', score_grads.astype(jnp.float32), window_keys.astype(jnp.float32)) * score_scale
        query_out = unrotate(query_grads, block_cosines, block_sines).astype(jnp.bfloat16).reshape(TOK_DEV, GROUP, KV_HEADS * HEAD)
        key_part = jnp.einsum('hgaw,aghd->whd', score_grads.astype(jnp.float32), rotated_queries.astype(jnp.float32)) * score_scale
        value_part = jnp.einsum('hgaw,aghd->whd', weights_low.astype(jnp.float32), grad_block.astype(jnp.float32))
        key_grads = lax.dynamic_update_slice_in_dim(key_grads, lax.dynamic_slice_in_dim(key_grads, offset, window_len, 0) + key_part, offset, 0)
        value_grads = lax.dynamic_update_slice_in_dim(value_grads, lax.dynamic_slice_in_dim(value_grads, offset, window_len, 0) + value_part, offset, 0)
        return ((key_grads, value_grads), query_out)
    zeros_init = jnp.zeros((TOKENS + WINDOW, KV_HEADS, HEAD), jnp.float32)
    (key_grads, value_grads), query_outs = lax.scan(one_block, (zeros_init, zeros_init), jnp.arange(TOKENS // TOK_DEV, dtype=jnp.int32))
    grad_queries = query_outs.reshape(TOKENS, GROUP, KV_HEADS * HEAD)
    grad_keys = unrotate(key_grads[WINDOW:], cosines[:, None, :], sines[:, None, :]).astype(jnp.bfloat16).reshape(TOKENS, KV_HEADS * HEAD)
    grad_values = value_grads[WINDOW:].astype(jnp.bfloat16).reshape(TOKENS, KV_HEADS * HEAD)
    return (grad_queries, grad_keys, grad_values)
```

```python
import functools
import math

import jax
import jax.numpy as jnp
import numpy as np
from jax import lax
from jax.experimental import pallas as pl
from jax.experimental.pallas import tpu as pltpu
from jax.sharding import PartitionSpec as P

HEAD = 128
BLOCK = 128
BEHIND = 512
SPAN = BLOCK + BEHIND
CHUNK = 256
OWN_HEADS = 4

rope_theta = 500000.0
rope_factor = 128.0
initial_context = 8192.0
ramp_low = 1.0
ramp_high = 32.0
attention_factor = 1.0 + 0.1 * math.log(rope_factor)
score_scale = 1.0 / math.sqrt(HEAD)
exponent_scale = score_scale / math.log(2.0)
EXCLUDED = -1e30

MESH = pl.DeviceIdType.MESH
NT = (((1,), (1,)), ((), ()))


def yarn_frequencies():
    halves = HEAD // 2
    powers = rope_theta ** (-2.0 * np.arange(halves) / HEAD)
    turns = initial_context * powers / (2.0 * np.pi)
    blend = np.clip((turns - ramp_low) / (ramp_high - ramp_low), 0.0, 1.0)
    return jnp.asarray(powers * ((1.0 - blend) / rope_factor + blend), jnp.float32)


def rope_tables(positions):
    frequency = yarn_frequencies()
    frequency = jnp.concatenate([frequency, frequency])
    signs = jnp.where(jnp.arange(HEAD) < HEAD // 2, -1.0, 1.0).astype(jnp.float32)
    angles = positions.astype(jnp.float32)[:, None] * frequency[None, :]
    return attention_factor * jnp.cos(angles), signs[None, :] * (attention_factor * jnp.sin(angles))


def dot(a, b):
    return jnp.dot(a, b, preferred_element_type=jnp.float32)


def kernel(
    outer_count, inner_count, groups,
    q_ref, g_ref, k_ref, v_ref, cos_ref, sin_ref,
    dq_ref, dk_ref, dv_ref,
    qb, gb, kraw, kv, tab, bias, qr, ps, dss, kt, acc, rin, ysend, yin, dqs,
    local_sem, own_sem, xs_sem, xr_sem, ys_sem, yr_sem, cs_sem, cr_sem,
    gcs_sem, gcr_sem, gys_sem, gyr_sem, dql_sem, dqs_sem, dqr_sem,
):
    outer, inner, head = lax.axis_index("outer"), lax.axis_index("inner"), lax.axis_index("head")
    blocks = outer_count * inner_count
    block = outer * inner_count + inner
    core = lax.rem(inner, 2)
    other = 1 - head

    def at(distance):
        target = lax.rem(block + distance + blocks, blocks)
        return (lax.div(target, inner_count), lax.rem(target, inner_count), head)

    partner = (outer, inner, other)
    sibling = (outer, inner + 1 - 2 * core, head)
    rows = BLOCK * groups
    mine = head * (OWN_HEADS * HEAD)
    theirs = other * (OWN_HEADS * HEAD)

    def columns(base, h):
        return pl.ds(pl.multiple_of(base + h * HEAD, HEAD), HEAD)

    def remote(src, dst, send, recv, device):
        return pltpu.make_async_remote_copy(
            src_ref=src, dst_ref=dst, send_sem=send, recv_sem=recv, device_id=device, device_id_type=MESH
        )

    def own_q(h):
        return pltpu.make_async_copy(q_ref.at[:, columns(mine, h)], qb.at[0, h], own_sem.at[0, h])

    def own_g(h):
        return pltpu.make_async_copy(g_ref.at[:, columns(mine, h)], gb.at[0, h], own_sem.at[1, h])

    def own_v(h):
        return pltpu.make_async_copy(v_ref.at[:, columns(mine, h)], kv.at[h, 4, 1], local_sem.at[h])

    def own_k():
        return pltpu.make_async_copy(
            k_ref.at[:, pl.ds(pl.multiple_of(mine, HEAD), OWN_HEADS * HEAD)], kraw, local_sem.at[OWN_HEADS]
        )

    def x_q(h):
        return remote(q_ref.at[:, columns(theirs, h)], qb.at[1, h], xs_sem.at[0, h], xr_sem.at[0, h], partner)

    def x_g(h):
        return remote(g_ref.at[:, columns(theirs, h)], gb.at[1, h], xs_sem.at[1, h], xr_sem.at[1, h], partner)

    def y_kv(h, i):
        return remote(kv.at[h, 4], kv.at[h, 2 - 2 * i], ys_sem.at[h, i], yr_sem.at[h, i], at(2 * i + 2))

    def c_kv(h, i):
        return remote(
            kv.at[h, 4 - 2 * core - 2 * i], kv.at[h, 3 - 2 * i], cs_sem.at[h, i], cr_sem.at[h, i], sibling
        )

    def c_grad(h, i):
        return remote(acc.at[h, 3 - 2 * i], rin.at[h, i], gcs_sem.at[h, i], gcr_sem.at[h, i], sibling)

    def y_grad(h, i):
        return remote(ysend.at[h, i], yin.at[h, i], gys_sem.at[h, i], gyr_sem.at[h, i], at(-2 * i - 2))

    def own_dq(h):
        return pltpu.make_async_copy(dqs.at[0, h], dq_ref.at[:, columns(mine, h)], dql_sem.at[h])

    def x_dq(h):
        return remote(dqs.at[1, h], dq_ref.at[:, columns(mine, h)], dqs_sem.at[h], dqr_sem.at[h], partner)

    def x_dq_arrival(h):
        return remote(dqs.at[1, h], dq_ref.at[:, columns(theirs, h)], dqs_sem.at[h], dqr_sem.at[h], partner)

    own_k().start()
    for h in range(OWN_HEADS):
        own_v(h).start()
    barrier = pltpu.get_barrier_semaphore()
    peers = (partner, sibling, at(2), at(4), at(-2), at(-4))
    for peer in peers:
        pl.semaphore_signal(barrier, inc=1, device_id=peer, device_id_type=MESH)
    for h in range(OWN_HEADS):
        own_q(h).start()
        own_g(h).start()

    cosines, sines = cos_ref[...], sin_ref[...]
    own_k().wait()
    for h in range(OWN_HEADS):
        raw = kraw[:, h * HEAD:(h + 1) * HEAD].astype(jnp.float32)
        kv[h, 4, 0] = (raw * cosines + pltpu.roll(raw, HEAD // 2, 1) * sines).astype(jnp.bfloat16)
    for h in range(OWN_HEADS):
        own_v(h).wait()

    pl.semaphore_wait(barrier, len(peers))
    for h in range(OWN_HEADS):
        for i in range(2):
            y_kv(h, i).start()
        x_q(h).start()
        x_g(h).start()

    low = lax.broadcasted_iota(jnp.int32, (8, HEAD), 0) < 4
    for table, ref in ((0, cos_ref), (1, sin_ref)):
        for pair in range(BLOCK // 2):
            first = jnp.broadcast_to(ref[2 * pair:2 * pair + 1, :], (8, HEAD))
            second = jnp.broadcast_to(ref[2 * pair + 1:2 * pair + 2, :], (8, HEAD))
            tab[table, 8 * pair:8 * pair + 8, :] = jnp.where(low, first, second)
    for part in (0, 1):
        row = lax.broadcasted_iota(jnp.int32, (SPAN - 64, CHUNK), 0)
        token = lax.broadcasted_iota(jnp.int32, (SPAN - 64, CHUNK), 1) // groups
        allowed = (row > token) & (row <= token + BEHIND) & (block * BLOCK - BEHIND + 64 * part + row >= 0)
        bias[part] = jnp.where(allowed, 0.0, EXCLUDED).astype(jnp.float32)
    for low_precision in (ps, dss):
        low_precision[SPAN - 64:, :CHUNK] = jnp.zeros((64, CHUNK), jnp.bfloat16)
        low_precision[:64, CHUNK:] = jnp.zeros((64, CHUNK), jnp.bfloat16)

    def stage(h):
        for i in range(2):
            y_kv(h, i).wait_recv()
        for i in range(2):
            c_kv(h, i).start()

    def unit(h, source):
        raw = qb[source, h].astype(jnp.float32)
        rotated = (raw * tab[0] + pltpu.roll(raw, HEAD // 2, 1) * tab[1]).astype(jnp.bfloat16)
        qr[...] = rotated
        keys = kv[h, :, 0].reshape(SPAN, HEAD)
        values = kv[h, :, 1].reshape(SPAN, HEAD)
        for part in (0, 1):
            here = slice(CHUNK * part, CHUNK * part + CHUNK)
            seen = slice(64 * part, 64 * part + SPAN - 64)
            scores = lax.dot_general(keys[seen], qr[here], NT, preferred_element_type=jnp.float32) + bias[part]
            top = jnp.max(scores, 0, keepdims=True)
            raised = jnp.exp2((scores - top) * exponent_scale)
            weights = raised * (1.0 / jnp.sum(raised, 0, keepdims=True))
            grads = lax.dot_general(values[seen], gb[source, h, here], NT, preferred_element_type=jnp.float32)
            delta = jnp.sum(weights * grads, 0, keepdims=True)
            ps[seen, here] = weights.astype(jnp.bfloat16)
            dss[seen, here] = (weights * (grads - delta)).astype(jnp.bfloat16)
        key_part = dot(dss[...], qr[...]).reshape(5, BLOCK, HEAD)
        value_part = dot(ps[...], gb[source, h]).reshape(5, BLOCK, HEAD)
        if source == 0:
            acc[h, :, 0] = key_part
            acc[h, :, 1] = value_part
        else:
            acc[h, :, 0] += key_part
            acc[h, :, 1] += value_part
        query_part = dot(kt[...], dss[...]).T
        query_part = query_part * score_scale
        dqs[source, h] = (query_part * tab[0] - pltpu.roll(query_part, HEAD // 2, 1) * tab[1]).astype(jnp.bfloat16)

    def combine(h):
        for i in range(2):
            c_grad(h, i).wait_recv()
            slot = 4 - 2 * core - 2 * i
            acc[h, slot] += rin[h, i]
        for i in range(2):
            ysend[h, i] = acc[h, 2 - 2 * i].astype(jnp.bfloat16)
            y_grad(h, i).start()

    stage(0)

    @pl.loop(0, OWN_HEADS)
    def _(h):
        for i in range(2):
            c_kv(h, i).wait_recv()
        kt[...] = kv[h, :, 0].reshape(SPAN, HEAD).T
        own_q(h).wait()
        own_g(h).wait()
        unit(h, 0)
        own_dq(h).start()

        @pl.when(h + 1 < OWN_HEADS)
        def _():
            stage(h + 1)

        @pl.when(h > 0)
        def _():
            combine(h - 1)

        x_q(h).wait_recv()
        x_g(h).wait_recv()
        unit(h, 1)
        for i in range(2):
            c_grad(h, i).start()
        x_dq(h).start()

    combine(OWN_HEADS - 1)
    for h in range(OWN_HEADS):
        for i in range(2):
            y_grad(h, i).wait_recv()
        total = acc[h, 4] + yin[h, 0].astype(jnp.float32) + yin[h, 1].astype(jnp.float32)
        key_total = total[0] * score_scale
        dk_ref[:, h * HEAD:(h + 1) * HEAD] = (
            key_total * cosines - pltpu.roll(key_total, HEAD // 2, 1) * sines
        ).astype(jnp.bfloat16)
        dv_ref[:, h * HEAD:(h + 1) * HEAD] = total[1].astype(jnp.bfloat16)

    for h in range(OWN_HEADS):
        x_q(h).wait_send()
        x_g(h).wait_send()
        own_dq(h).wait()
        x_dq(h).wait_send()
        x_dq_arrival(h).wait_recv()
        for i in range(2):
            y_kv(h, i).wait_send()
            c_kv(h, i).wait_send()
            c_grad(h, i).wait_send()
            y_grad(h, i).wait_send()


def body(outer_count, inner_count, queries, keys, values, grad_out, positions):
    tokens, groups, width = queries.shape
    rows = tokens * groups
    half = OWN_HEADS * HEAD
    cosines, sines = rope_tables(positions)
    low, high = jnp.bfloat16, jnp.float32
    semaphores = pltpu.SemaphoreType.DMA
    pairs = (OWN_HEADS, 2)
    anywhere = pl.BlockSpec(memory_space=pl.ANY)
    on_chip = pl.BlockSpec(memory_space=pltpu.VMEM)
    dq, dk, dv = pl.pallas_call(
        functools.partial(kernel, outer_count, inner_count, groups),
        out_shape=(
            jax.ShapeDtypeStruct((rows, width), low),
            jax.ShapeDtypeStruct((tokens, half), low),
            jax.ShapeDtypeStruct((tokens, half), low),
        ),
        in_specs=[anywhere] * 4 + [on_chip] * 2,
        out_specs=(anywhere, on_chip, on_chip),
        scratch_shapes=[
            pltpu.VMEM((2, OWN_HEADS, rows, HEAD), low),
            pltpu.VMEM((2, OWN_HEADS, rows, HEAD), low),
            pltpu.VMEM((tokens, half), low),
            pltpu.VMEM((OWN_HEADS, 5, 2, BLOCK, HEAD), low),
            pltpu.VMEM((2, rows, HEAD), high),
            pltpu.VMEM((2, SPAN - 64, CHUNK), high),
            pltpu.VMEM((rows, HEAD), low),
            pltpu.VMEM((SPAN, rows), low),
            pltpu.VMEM((SPAN, rows), low),
            pltpu.VMEM((HEAD, SPAN), low),
            pltpu.VMEM((OWN_HEADS, 5, 2, BLOCK, HEAD), high),
            pltpu.VMEM((OWN_HEADS, 2, 2, BLOCK, HEAD), high),
            pltpu.VMEM((OWN_HEADS, 2, 2, BLOCK, HEAD), low),
            pltpu.VMEM((OWN_HEADS, 2, 2, BLOCK, HEAD), low),
            pltpu.VMEM((2, OWN_HEADS, rows, HEAD), low),
            semaphores((OWN_HEADS + 1,)),
            semaphores((2, OWN_HEADS)),
            semaphores((2, OWN_HEADS)),
            semaphores((2, OWN_HEADS)),
            semaphores(pairs),
            semaphores(pairs),
            semaphores(pairs),
            semaphores(pairs),
            semaphores(pairs),
            semaphores(pairs),
            semaphores(pairs),
            semaphores(pairs),
            semaphores((OWN_HEADS,)),
            semaphores((OWN_HEADS,)),
            semaphores((OWN_HEADS,)),
        ],
        compiler_params=pltpu.CompilerParams(collective_id=0, has_side_effects=True, vmem_limit_bytes=48 * 2**20),
    )(
        queries.reshape(rows, width),
        grad_out.reshape(rows, width),
        keys,
        values,
        cosines,
        sines,
    )
    return dq.reshape(tokens, groups, width), dk, dv


def solution(mesh):
    placed = (
        P(("outer", "inner"), "head", None),
        P(("outer", "inner"), None),
        P(("outer", "inner"), None),
        P(("outer", "inner"), "head", None),
        P(("outer", "inner")),
    )
    return jax.shard_map(
        functools.partial(body, mesh.shape["outer"], mesh.shape["inner"]),
        mesh=mesh,
        in_specs=placed,
        out_specs=(
            P(("outer", "inner"), "head", None),
            P(("outer", "inner"), "head"),
            P(("outer", "inner"), "head"),
        ),
        check_vma=False,
    )
```

```python
import functools
import math

import jax
import jax.numpy as jnp
import numpy as np
from jax import lax
from jax.experimental import pallas as pl
from jax.experimental.pallas import tpu as pltpu
from jax.sharding import PartitionSpec as P

HEAD = 128
BLOCK = 128
BEHIND = 512
SPAN = BLOCK + BEHIND
CHUNK = 256
OWN_HEADS = 4
SHARED = 1
PLACES = OWN_HEADS + SHARED

rope_theta = 500000.0
rope_factor = 128.0
initial_context = 8192.0
ramp_low = 1.0
ramp_high = 32.0
attention_factor = 1.0 + 0.1 * math.log(rope_factor)
score_scale = 1.0 / math.sqrt(HEAD)
exponent_scale = score_scale / math.log(2.0)
EXCLUDED = -1e30

MESH = pl.DeviceIdType.MESH
NT = (((1,), (1,)), ((), ()))


def yarn_frequencies():
    halves = HEAD // 2
    powers = rope_theta ** (-2.0 * np.arange(halves) / HEAD)
    turns = initial_context * powers / (2.0 * np.pi)
    blend = np.clip((turns - ramp_low) / (ramp_high - ramp_low), 0.0, 1.0)
    return jnp.asarray(powers * ((1.0 - blend) / rope_factor + blend), jnp.float32)


def rope_tables(positions):
    frequency = yarn_frequencies()
    frequency = jnp.concatenate([frequency, frequency])
    signs = jnp.where(jnp.arange(HEAD) < HEAD // 2, -1.0, 1.0).astype(jnp.float32)
    angles = positions.astype(jnp.float32)[:, None] * frequency[None, :]
    return attention_factor * jnp.cos(angles), signs[None, :] * (attention_factor * jnp.sin(angles))


def dot(a, b):
    return jnp.dot(a, b, preferred_element_type=jnp.float32)


def kernel(
    outer_count, inner_count, groups,
    q_ref, g_ref, k_ref, v_ref, cos_ref, sin_ref,
    dq_ref, dk_ref, dv_ref,
    qb, gb, qr, kraw, kv, tab, bias, ps, dss, kt, acc, rin, ysend, yin, dqs, fsend, fin, done,
    k_sem, v_sem, q_sem, g_sem, xs_sem, xr_sem, ys_sem, yr_sem, cs_sem, cr_sem,
    gcs_sem, gcr_sem, gys_sem, gyr_sem, dql_sem, dqs_sem, dqr_sem, fs_sem, fr_sem, os_sem, or_sem,
):
    outer, inner, head = lax.axis_index("outer"), lax.axis_index("inner"), lax.axis_index("head")
    blocks = outer_count * inner_count
    half_outer = outer_count // 2
    block = outer * inner_count + inner
    core = lax.rem(inner, 2)
    flip = lax.div(outer, half_outer)
    owner = lax.rem(head + flip, 2)

    def at(distance):
        target = lax.rem(block + distance + blocks, blocks)
        target_outer = lax.div(target, inner_count)
        target_head = lax.rem(owner + lax.div(target_outer, half_outer), 2)
        return (target_outer, lax.rem(target, inner_count), target_head)

    partner = (outer, inner, 1 - head)
    sibling = (outer, inner + 1 - 2 * core, head)
    ahead, back = at(2), at(-2)
    mine = owner * (OWN_HEADS * HEAD)
    theirs = (1 - owner) * (OWN_HEADS * HEAD)

    def columns(start):
        return pl.ds(pl.multiple_of(start, HEAD), HEAD)

    def column_of(p):
        if isinstance(p, int):
            return theirs + p * HEAD if p < SHARED else mine + (p - SHARED) * HEAD
        kept = lax.min(lax.div(p, SHARED), 1) if SHARED else 1
        return theirs + p * HEAD + kept * (mine - theirs - SHARED * HEAD)

    def local(src, dst, sem):
        return pltpu.make_async_copy(src, dst, sem)

    def remote(src, dst, send, recv, device):
        return pltpu.make_async_remote_copy(
            src_ref=src, dst_ref=dst, send_sem=send, recv_sem=recv, device_id=device, device_id_type=MESH
        )

    def own_k(p):
        return local(k_ref.at[:, columns(column_of(p))], kraw.at[p], k_sem.at[p])

    def own_v(p):
        return local(v_ref.at[:, columns(column_of(p))], kv.at[p, 4, 1], v_sem.at[p])

    def own_q(p):
        return local(q_ref.at[:, columns(column_of(p))], qb.at[p], q_sem.at[p])

    def own_g(p):
        return local(g_ref.at[:, columns(column_of(p))], gb.at[p], g_sem.at[p])

    def x_q(p):
        n = p - 2 * SHARED
        return remote(
            q_ref.at[:, columns(theirs + (p - SHARED) * HEAD)], qb.at[PLACES + n], xs_sem.at[0, n], xr_sem.at[0, n], partner
        )

    def x_g(p):
        n = p - 2 * SHARED
        return remote(
            g_ref.at[:, columns(theirs + (p - SHARED) * HEAD)], gb.at[PLACES + n], xs_sem.at[1, n], xr_sem.at[1, n], partner
        )

    def y_kv(p, i):
        return remote(kv.at[p, 4 - 2 * i], kv.at[p, 2 - 2 * i], ys_sem.at[p, i], yr_sem.at[p, i], ahead)

    def c_kv(p, i):
        return remote(
            kv.at[p, 4 - 2 * core - 2 * i], kv.at[p, 3 - 2 * i], cs_sem.at[p, i], cr_sem.at[p, i], sibling
        )

    def c_grad(p, i):
        return remote(acc.at[p, 3 - 2 * i], rin.at[p, i], gcs_sem.at[p, i], gcr_sem.at[p, i], sibling)

    def y_grad(p, i):
        return remote(ysend.at[p, i], yin.at[p, i], gys_sem.at[p, i], gyr_sem.at[p, i], back)

    def own_dq(p):
        return local(dqs.at[p], dq_ref.at[:, columns(column_of(p))], dql_sem.at[p])

    def x_dq(p, start):
        n = p - 2 * SHARED
        return remote(
            dqs.at[PLACES + n], dq_ref.at[:, columns(start + (p - SHARED) * HEAD)], dqs_sem.at[n], dqr_sem.at[n], partner
        )

    def x_shared(i):
        return remote(fsend.at[i], fin.at[i], fs_sem.at[i], fr_sem.at[i], partner)

    def results(p):
        here = pl.ds((p - SHARED) * HEAD, HEAD)
        return ((done.at[p, 0], dk_ref.at[:, here]), (done.at[p, 1], dv_ref.at[:, here]))

    def own_out(p, i):
        src, dst = results(p)[i]
        return local(src, dst, os_sem.at[p, i])

    def x_out(p, i):
        src, dst = results(p)[i]
        return remote(src, dst, os_sem.at[p, i], or_sem.at[p, i], partner)

    for p in range(PLACES):
        own_k(p).start()
        own_v(p).start()
    barrier = pltpu.get_barrier_semaphore()
    peers = (partner, sibling, ahead, back)
    for peer in peers:
        pl.semaphore_signal(barrier, inc=1, device_id=peer, device_id_type=MESH)
    for p in range(PLACES):
        own_q(p).start()
        own_g(p).start()

    cosines, sines = cos_ref[...], sin_ref[...]
    for p in range(PLACES):
        own_k(p).wait()
        raw = kraw[p].astype(jnp.float32)
        kv[p, 4, 0] = (raw * cosines + pltpu.roll(raw, HEAD // 2, 1) * sines).astype(jnp.bfloat16)
    for p in range(PLACES):
        own_v(p).wait()

    pl.semaphore_wait(barrier, len(peers))
    for p in range(2):
        y_kv(p, 0).start()
    for p in range(2 * SHARED, PLACES):
        x_q(p).start()
        x_g(p).start()

    def stage_a(p):
        y_kv(p, 0).wait_recv()
        y_kv(p, 1).start()
        if isinstance(p, int):
            y_kv(p + 2, 0).start()
        else:
            @pl.when(p + 2 < PLACES)
            def _():
                y_kv(p + 2, 0).start()
        c_kv(p, 0).start()

    def stage_b(p):
        y_kv(p, 1).wait_recv()
        c_kv(p, 1).start()

    low = lax.broadcasted_iota(jnp.int32, (8, HEAD), 0) < 4
    for table, ref in ((0, cos_ref), (1, sin_ref)):
        for pair in range(BLOCK // 2):
            first = jnp.broadcast_to(ref[2 * pair:2 * pair + 1, :], (8, HEAD))
            second = jnp.broadcast_to(ref[2 * pair + 1:2 * pair + 2, :], (8, HEAD))
            tab[table, 8 * pair:8 * pair + 8, :] = jnp.where(low, first, second)

    stage_a(0)
    for part in (0, 1):
        row = lax.broadcasted_iota(jnp.int32, (SPAN - 64, CHUNK), 0)
        token = lax.broadcasted_iota(jnp.int32, (SPAN - 64, CHUNK), 1) // groups
        allowed = (row > token) & (row <= token + BEHIND) & (block * BLOCK - BEHIND + 64 * part + row >= 0)
        bias[part] = jnp.where(allowed, 0.0, EXCLUDED).astype(jnp.float32)
    for low_precision in (ps, dss):
        low_precision[SPAN - 64:, :CHUNK] = jnp.zeros((64, CHUNK), jnp.bfloat16)
        low_precision[:64, CHUNK:] = jnp.zeros((64, CHUNK), jnp.bfloat16)
    stage_a(1)

    def rotate_queries(n):
        raw = qb[n].astype(jnp.float32)
        qr[n] = (raw * tab[0] + pltpu.roll(raw, HEAD // 2, 1) * tab[1]).astype(jnp.bfloat16)

    @pl.loop(0, PLACES)
    def _(p):
        own_q(p).wait()
        own_g(p).wait()
        rotate_queries(p)

    stage_b(0)

    def unit(p, n, first):
        keys = kv[p, :, 0].reshape(SPAN, HEAD)
        values = kv[p, :, 1].reshape(SPAN, HEAD)
        for part in (0, 1):
            here = slice(CHUNK * part, CHUNK * part + CHUNK)
            seen = slice(64 * part, 64 * part + SPAN - 64)
            scores = lax.dot_general(keys[seen], qr[n, here], NT, preferred_element_type=jnp.float32) + bias[part]
            top = jnp.max(scores, 0, keepdims=True)
            raised = jnp.exp2((scores - top) * exponent_scale)
            weights = raised * (1.0 / jnp.sum(raised, 0, keepdims=True))
            grads = lax.dot_general(values[seen], gb[n, here], NT, preferred_element_type=jnp.float32)
            delta = jnp.sum(weights * grads, 0, keepdims=True)
            ps[seen, here] = weights.astype(jnp.bfloat16)
            dss[seen, here] = (weights * (grads - delta)).astype(jnp.bfloat16)
        key_part = dot(dss[...], qr[n]).reshape(5, BLOCK, HEAD)
        value_part = dot(ps[...], gb[n]).reshape(5, BLOCK, HEAD)
        if first:
            acc[p, :, 0] = key_part
            acc[p, :, 1] = value_part
        else:
            acc[p, :, 0] += key_part
            acc[p, :, 1] += value_part
        query_part = dot(kt[...], dss[...]).T
        query_part = query_part * score_scale
        dqs[n] = (query_part * tab[0] - pltpu.roll(query_part, HEAD // 2, 1) * tab[1]).astype(jnp.bfloat16)

    def combine_a(p):
        for i in range(2):
            c_grad(p, i).wait_recv()
            acc[p, 4 - 2 * core - 2 * i] += rin[p, i]
        ysend[p, 1] = acc[p, 0].astype(jnp.bfloat16)
        y_grad(p, 1).start()

    def combine_b(p):
        y_grad(p, 1).wait_recv()
        ysend[p, 0] = (acc[p, 2] + yin[p, 1].astype(jnp.float32)).astype(jnp.bfloat16)
        y_grad(p, 0).start()

    def total_of(p):
        y_grad(p, 0).wait_recv()
        return acc[p, 4] + yin[p, 0].astype(jnp.float32)

    def send_shared():
        for i in range(SHARED):
            fsend[i] = total_of(flip * SHARED + i).astype(jnp.bfloat16)
            x_shared(i).start()

    def finish(p, total):
        key_total = total[0] * score_scale
        done[p, 0] = (key_total * cosines - pltpu.roll(key_total, HEAD // 2, 1) * sines).astype(jnp.bfloat16)
        done[p, 1] = total[1].astype(jnp.bfloat16)

    def finish_swapped(p):
        finish(p, total_of(p))

        @pl.when(flip == 0)
        def _():
            for i in range(2):
                own_out(p, i).start()

        @pl.when(flip == 1)
        def _():
            for i in range(2):
                x_out(p, i).start()

    def position(p, swapped):
        for i in range(2):
            c_kv(p, i).wait_recv()
        kt[...] = kv[p, :, 0].reshape(SPAN, HEAD).T

        @pl.when(p + 2 < PLACES)
        def _():
            stage_a(p + 2)

        unit(p, p, True)
        own_dq(p).start()
        if not swapped:
            for i in range(2):
                c_grad(p, i).start()

        @pl.when(p + 1 < PLACES)
        def _():
            stage_b(p + 1)

        @pl.when(p > 0)
        def _():
            combine_a(p - 1)

        @pl.when(p > 1)
        def _():
            combine_b(p - 2)

        if swapped:
            if early_shared:
                @pl.when(p == PLACES - 1)
                def _():
                    send_shared()
            n = PLACES + p - 2 * SHARED
            x_q(p).wait_recv()
            x_g(p).wait_recv()
            rotate_queries(n)
            unit(p, n, False)
            for i in range(2):
                c_grad(p, i).start()
            x_dq(p, mine).start()

    early_shared = 2 * SHARED + 2 < PLACES
    if SHARED:
        @pl.loop(0, 2 * SHARED)
        def _(p):
            position(p, False)

    @pl.loop(2 * SHARED, PLACES)
    def _(p):
        position(p, True)

    combine_a(PLACES - 1)
    combine_b(PLACES - 2)
    if not early_shared:
        send_shared()
    for p in range(2 * SHARED, PLACES - 2):
        finish_swapped(p)
    combine_b(PLACES - 1)
    for p in range(max(2 * SHARED, PLACES - 2), PLACES - 1):
        finish_swapped(p)
    for i in range(SHARED):
        p = (1 - flip) * SHARED + i
        total = total_of(p)
        x_shared(i).wait_recv()
        finish(SHARED + i, total + fin[i].astype(jnp.float32))
        for o in range(2):
            own_out(SHARED + i, o).start()
    finish_swapped(PLACES - 1)

    for p in range(PLACES):
        own_dq(p).wait()
        for i in range(2):
            y_kv(p, i).wait_send()
            c_kv(p, i).wait_send()
            c_grad(p, i).wait_send()
            y_grad(p, i).wait_send()
    for i in range(SHARED):
        x_shared(i).wait_send()
        for o in range(2):
            own_out(SHARED + i, o).wait()
    for p in range(2 * SHARED, PLACES):
        x_q(p).wait_send()
        x_g(p).wait_send()
        x_dq(p, mine).wait_send()
        x_dq(p, theirs).wait_recv()

    @pl.when(flip == 0)
    def _():
        for p in range(2 * SHARED, PLACES):
            for i in range(2):
                own_out(p, i).wait()

    @pl.when(flip == 1)
    def _():
        for p in range(2 * SHARED, PLACES):
            for i in range(2):
                x_out(p, i).wait_send()
                x_out(p, i).wait_recv()


def body(outer_count, inner_count, queries, keys, values, grad_out, positions):
    tokens, groups, width = queries.shape
    rows = tokens * groups
    half = OWN_HEADS * HEAD
    cosines, sines = rope_tables(positions)
    low, high = jnp.bfloat16, jnp.float32
    semaphores = pltpu.SemaphoreType.DMA
    swapped = OWN_HEADS - SHARED
    pairs = (PLACES, 2)
    anywhere = pl.BlockSpec(memory_space=pl.ANY)
    off_chip = pl.BlockSpec(memory_space=pltpu.HBM)
    on_chip = pl.BlockSpec(memory_space=pltpu.VMEM)
    dq, dk, dv = pl.pallas_call(
        functools.partial(kernel, outer_count, inner_count, groups),
        out_shape=(
            jax.ShapeDtypeStruct((rows, width), low),
            jax.ShapeDtypeStruct((tokens, half), low),
            jax.ShapeDtypeStruct((tokens, half), low),
        ),
        in_specs=[anywhere] * 2 + [off_chip] * 2 + [on_chip] * 2,
        out_specs=(anywhere, off_chip, off_chip),
        scratch_shapes=[
            pltpu.VMEM((2 * OWN_HEADS, rows, HEAD), low),
            pltpu.VMEM((2 * OWN_HEADS, rows, HEAD), low),
            pltpu.VMEM((2 * OWN_HEADS, rows, HEAD), low),
            pltpu.VMEM((PLACES, tokens, HEAD), low),
            pltpu.VMEM((PLACES, 5, 2, BLOCK, HEAD), low),
            pltpu.VMEM((2, rows, HEAD), high),
            pltpu.VMEM((2, SPAN - 64, CHUNK), high),
            pltpu.VMEM((SPAN, rows), low),
            pltpu.VMEM((SPAN, rows), low),
            pltpu.VMEM((HEAD, SPAN), low),
            pltpu.VMEM((PLACES, 5, 2, BLOCK, HEAD), high),
            pltpu.VMEM((PLACES, 2, 2, BLOCK, HEAD), high),
            pltpu.VMEM((PLACES, 2, 2, BLOCK, HEAD), low),
            pltpu.VMEM((PLACES, 2, 2, BLOCK, HEAD), low),
            pltpu.VMEM((2 * OWN_HEADS, rows, HEAD), low),
            pltpu.VMEM((max(SHARED, 1), 2, BLOCK, HEAD), low),
            pltpu.VMEM((max(SHARED, 1), 2, BLOCK, HEAD), low),
            pltpu.VMEM((PLACES, 2, BLOCK, HEAD), low),
            semaphores((PLACES,)),
            semaphores((PLACES,)),
            semaphores((PLACES,)),
            semaphores((PLACES,)),
            semaphores((2, swapped)),
            semaphores((2, swapped)),
            semaphores(pairs),
            semaphores(pairs),
            semaphores(pairs),
            semaphores(pairs),
            semaphores(pairs),
            semaphores(pairs),
            semaphores(pairs),
            semaphores(pairs),
            semaphores((PLACES,)),
            semaphores((swapped,)),
            semaphores((swapped,)),
            semaphores((max(SHARED, 1),)),
            semaphores((max(SHARED, 1),)),
            semaphores(pairs),
            semaphores(pairs),
        ],
        compiler_params=pltpu.CompilerParams(collective_id=0, has_side_effects=True, vmem_limit_bytes=48 * 2**20),
    )(
        queries.reshape(rows, width),
        grad_out.reshape(rows, width),
        keys,
        values,
        cosines,
        sines,
    )
    return dq.reshape(tokens, groups, width), dk, dv


def solution(mesh):
    placed = (
        P(("outer", "inner"), "head", None),
        P(("outer", "inner"), None),
        P(("outer", "inner"), None),
        P(("outer", "inner"), "head", None),
        P(("outer", "inner")),
    )
    return jax.shard_map(
        functools.partial(body, mesh.shape["outer"], mesh.shape["inner"]),
        mesh=mesh,
        in_specs=placed,
        out_specs=(
            P(("outer", "inner"), "head", None),
            P(("outer", "inner"), "head"),
            P(("outer", "inner"), "head"),
        ),
        check_vma=False,
    )
```

```python
import functools
import math

import jax
import jax.numpy as jnp
import numpy as np
from jax import lax
from jax.experimental import pallas as pl
from jax.experimental.pallas import tpu as pltpu
from jax.sharding import PartitionSpec as P

HEAD = 128
BLOCK = 128
BEHIND = 512
SPAN = BLOCK + BEHIND
CHUNK = 256
OWN_HEADS = 4
PLACES = OWN_HEADS
SETTLE = 4

rope_theta = 500000.0
rope_factor = 128.0
initial_context = 8192.0
ramp_low = 1.0
ramp_high = 32.0
attention_factor = 1.0 + 0.1 * math.log(rope_factor)
score_scale = 1.0 / math.sqrt(HEAD)
exponent_scale = score_scale / math.log(2.0)
EXCLUDED = -1e30

MESH = pl.DeviceIdType.MESH
NT = (((1,), (1,)), ((), ()))


def yarn_frequencies():
    halves = HEAD // 2
    powers = rope_theta ** (-2.0 * np.arange(halves) / HEAD)
    turns = initial_context * powers / (2.0 * np.pi)
    blend = np.clip((turns - ramp_low) / (ramp_high - ramp_low), 0.0, 1.0)
    return np.asarray(powers * ((1.0 - blend) / rope_factor + blend), np.float32)


TURN_HIGH = 6.28125
TURN_MIDDLE = math.floor((2.0 * math.pi - TURN_HIGH) * 2.0**20) / 2.0**20
TURN_LOW = 2.0 * math.pi - TURN_HIGH - TURN_MIDDLE


def rope_tables(positions):
    lane = lax.broadcasted_iota(jnp.int32, (8, HEAD), 1)
    frequency = jnp.zeros((8, HEAD), jnp.float32)
    for index, value in enumerate(yarn_frequencies()):
        frequency = jnp.where(lax.rem(lane, HEAD // 2) == index, float(value), frequency)
    times = jnp.broadcast_to(positions.astype(jnp.float32), (BLOCK, HEAD)).T
    angles = times * frequency[0:1]
    turns = jnp.floor(angles * (0.5 / math.pi) + 0.5)
    rest = ((angles - turns * TURN_HIGH) - turns * TURN_MIDDLE) - turns * TURN_LOW
    signed = jnp.where(lane[0:1] < HEAD // 2, -attention_factor, attention_factor)
    return attention_factor * jnp.cos(rest), signed * jnp.sin(rest)


def dot(a, b):
    return jnp.dot(a, b, preferred_element_type=jnp.float32)


def kernel(
    outer_count, inner_count, groups,
    q_ref, g_ref, k_ref, v_ref, pos_ref,
    dq_ref, dkv_ref,
    qb, gb, qr, gr, kraw, kv, pos, small, tab, bias, ps, dss, kt, acc, rin, ysend, yin, dqs, done,
    pos_sem, k_sem, v_sem, q_sem, g_sem, xs_sem, xr_sem, ys_sem, yr_sem, cs_sem, cr_sem,
    gcs_sem, gcr_sem, gys_sem, gyr_sem, dql_sem, dqs_sem, dqr_sem, os_sem, or_sem,
):
    outer, inner, head = lax.axis_index("outer"), lax.axis_index("inner"), lax.axis_index("head")
    blocks = outer_count * inner_count
    half_outer = outer_count // 2
    block = outer * inner_count + inner
    core = lax.rem(inner, 2)
    later = lax.div(outer, half_outer)
    flip = 1 - later
    owner = lax.rem(head + flip, 2)
    first, last = block < 2, block >= blocks - 2
    has_back, has_ahead = block >= 2, block < blocks - 2

    def at(distance):
        target = lax.rem(block + distance + blocks, blocks)
        target_outer = lax.div(target, inner_count)
        target_head = lax.rem(owner + 1 - lax.div(target_outer, half_outer), 2)
        return (target_outer, lax.rem(target, inner_count), target_head)

    partner = (outer, inner, 1 - head)
    sibling = (outer, inner + 1 - 2 * core, head)
    ahead, back = at(2), at(-2)
    rows = BLOCK * groups
    mine = owner * (OWN_HEADS * HEAD)
    theirs = (1 - owner) * (OWN_HEADS * HEAD)

    def columns(start):
        return pl.ds(pl.multiple_of(start, HEAD), HEAD)

    def column_of(p):
        return mine + p * HEAD

    def local(src, dst, sem):
        return pltpu.make_async_copy(src, dst, sem)

    def remote(src, dst, send, recv, device):
        return pltpu.make_async_remote_copy(
            src_ref=src, dst_ref=dst, send_sem=send, recv_sem=recv, device_id=device, device_id_type=MESH
        )

    def own_k(p):
        return local(k_ref.at[:, columns(column_of(p))], kraw.at[p], k_sem.at[p])

    def own_v(p):
        return local(v_ref.at[:, columns(column_of(p))], kv.at[p, 4, 1], v_sem.at[p])

    def own_q(p):
        return local(q_ref.at[:, :, columns(column_of(p))], qb.at[p], q_sem.at[p])

    def own_g(p):
        return local(g_ref.at[:, :, columns(column_of(p))], gb.at[p], g_sem.at[p])

    def x_q(p):
        return remote(q_ref.at[:, :, columns(theirs + p * HEAD)], qb.at[PLACES + p], xs_sem.at[0, p], xr_sem.at[0, p], partner)

    def x_g(p):
        return remote(g_ref.at[:, :, columns(theirs + p * HEAD)], gb.at[PLACES + p], xs_sem.at[1, p], xr_sem.at[1, p], partner)

    def y_kv(p, i, kind):
        n = 2 * i + kind
        return remote(kv.at[p, 4 - 2 * i, kind], kv.at[p, 2 - 2 * i, kind], ys_sem.at[p, n], yr_sem.at[p, n], ahead)

    def c_kv(p, i, kind):
        n = 2 * i + kind
        src = kv.at[p, 4 - 2 * core - 2 * i, kind]
        return remote(src, kv.at[p, 3 - 2 * i, kind], cs_sem.at[p, n], cr_sem.at[p, n], sibling)

    def c_grad(p, i, kind):
        n = 2 * i + kind
        return remote(acc.at[p, 3 - 2 * i, kind], rin.at[p, i, kind], gcs_sem.at[p, n], gcr_sem.at[p, n], sibling)

    def y_grad(p, i, kind):
        n = 2 * i + kind
        return remote(ysend.at[p, i, kind], yin.at[p, i, kind], gys_sem.at[p, n], gyr_sem.at[p, n], back)

    def own_dq(p):
        return local(dqs.at[p], dq_ref.at[:, :, columns(column_of(p))], dql_sem.at[p])

    def x_dq(p, start):
        return remote(
            dqs.at[PLACES + p], dq_ref.at[:, :, columns(start + p * HEAD)], dqs_sem.at[p], dqr_sem.at[p], partner
        )

    def results(p):
        here = pl.ds(p * HEAD, HEAD)
        return ((done.at[p, 0], dkv_ref.at[0, :, here]), (done.at[p, 1], dkv_ref.at[1, :, here]))

    def own_out(p, i):
        src, dst = results(p)[i]
        return local(src, dst, os_sem.at[p, i])

    def x_out(p, i):
        src, dst = results(p)[i]
        return remote(src, dst, os_sem.at[p, i], or_sem.at[p, i], partner)

    times = local(pos_ref, pos, pos_sem)
    times.start()
    for p in range(PLACES):
        own_k(p).start()
        own_v(p).start()
    barrier = pltpu.get_barrier_semaphore()

    def greet(peer):
        pl.semaphore_signal(barrier, inc=1, device_id=peer, device_id_type=MESH)

    greet(partner)
    greet(sibling)

    @pl.when(has_ahead)
    def _():
        greet(ahead)

    @pl.when(has_back)
    def _():
        greet(back)

    times.wait()
    small[0], small[1] = rope_tables(pos[...])
    cosines, sines = small[0], small[1]
    for p in range(PLACES):
        own_k(p).wait()
        raw = kraw[p].astype(jnp.float32)
        kv[p, 4, 0] = (raw * cosines + pltpu.roll(raw, HEAD // 2, 1) * sines).astype(jnp.bfloat16)
    for p in range(PLACES):
        own_v(p).wait()
    @pl.when(has_ahead & has_back)
    def _():
        pl.semaphore_wait(barrier, 4)

    @pl.when(first | last)
    def _():
        pl.semaphore_wait(barrier, 3)

    @pl.when(first)
    def _():
        for p in range(PLACES):
            kv[p, 0] = jnp.zeros((2, BLOCK, HEAD), jnp.bfloat16)
            kv[p, 2] = jnp.zeros((2, BLOCK, HEAD), jnp.bfloat16)

    @pl.when(last)
    def _():
        yin[...] = jnp.zeros(yin.shape, jnp.bfloat16)


    def send_own(p):
        @pl.when(has_ahead)
        def _():
            for kind in range(2):
                y_kv(p, 0, kind).start()

    send_own(0)
    send_own(1)
    for p in range(PLACES):
        x_q(p).start()
        x_g(p).start()
    for p in range(PLACES):
        own_q(p).start()
        own_g(p).start()

    def stage_a(p):
        for kind in range(2):
            @pl.when(has_back)
            def _():
                y_kv(p, 0, kind).wait_recv()

            @pl.when(has_ahead)
            def _():
                y_kv(p, 1, kind).start()

            c_kv(p, 0, kind).start()

        @pl.when(p + 2 < PLACES)
        def _():
            send_own(p + 2)

    def stage_b(p):
        for kind in range(2):
            @pl.when(has_back)
            def _():
                y_kv(p, 1, kind).wait_recv()

            c_kv(p, 1, kind).start()

    low = lax.broadcasted_iota(jnp.int32, (8, HEAD), 0) < 4
    for table in (0, 1):
        for pair in range(BLOCK // 2):
            first = jnp.broadcast_to(small[table, 2 * pair:2 * pair + 1, :], (8, HEAD))
            second = jnp.broadcast_to(small[table, 2 * pair + 1:2 * pair + 2, :], (8, HEAD))
            tab[table, 8 * pair:8 * pair + 8, :] = jnp.where(low, first, second)

    stage_a(0)
    for part in (0, 1):
        row = lax.broadcasted_iota(jnp.int32, (SPAN - 64, CHUNK), 0)
        token = lax.broadcasted_iota(jnp.int32, (SPAN - 64, CHUNK), 1) // groups
        allowed = (row > token) & (row <= token + BEHIND) & (block * BLOCK - BEHIND + 64 * part + row >= 0)
        bias[part] = jnp.where(allowed, 0.0, EXCLUDED).astype(jnp.float32)
    for low_precision in (ps, dss):
        for side in (0, 2 * CHUNK):
            low_precision[SPAN - 64:, side:side + CHUNK] = jnp.zeros((64, CHUNK), jnp.bfloat16)
            low_precision[:64, side + CHUNK:side + 2 * CHUNK] = jnp.zeros((64, CHUNK), jnp.bfloat16)
    stage_a(1)

    def rotate_queries(n, side):
        raw = qb[n].reshape(rows, HEAD).astype(jnp.float32)
        gr[side] = gb[n].reshape(rows, HEAD)
        qr[side] = (raw * tab[0] + pltpu.roll(raw, HEAD // 2, 1) * tab[1]).astype(jnp.bfloat16)

    own_q(0).wait()
    own_g(0).wait()
    rotate_queries(0, 0)
    stage_b(0)

    def weigh(p, n, side):
        keys = kv[p, :, 0].reshape(SPAN, HEAD)
        values = kv[p, :, 1].reshape(SPAN, HEAD)
        for part in (0, 1):
            here = slice(CHUNK * part, CHUNK * part + CHUNK)
            there = slice(rows * side + CHUNK * part, rows * side + CHUNK * part + CHUNK)
            seen = slice(64 * part, 64 * part + SPAN - 64)
            scores = lax.dot_general(keys[seen], qr[side, here], NT, preferred_element_type=jnp.float32) + bias[part]
            top = jnp.max(scores, 0, keepdims=True)
            raised = jnp.exp2((scores - top) * exponent_scale)
            weights = raised * (1.0 / jnp.sum(raised, 0, keepdims=True))
            grads = lax.dot_general(values[seen], gr[side, here], NT, preferred_element_type=jnp.float32)
            delta = jnp.sum(weights * grads, 0, keepdims=True)
            ps[seen, there] = weights.astype(jnp.bfloat16)
            dss[seen, there] = (weights * (grads - delta)).astype(jnp.bfloat16)

    def query_grads(n, side):
        query_part = dot(kt[...], dss[:, rows * side:rows * side + rows]).T
        query_part = query_part * score_scale
        rotated = query_part * tab[0] - pltpu.roll(query_part, HEAD // 2, 1) * tab[1]
        dqs[n] = rotated.astype(jnp.bfloat16).reshape(BLOCK, groups, HEAD)

    def key_grads(p):
        for kind, weights, vectors in ((1, ps, gr), (0, dss, qr)):
            acc[p, :, kind] = dot(weights[...], vectors[...].reshape(2 * rows, HEAD)).reshape(5, BLOCK, HEAD)
            for i in range(2):
                c_grad(p, i, kind).start()

    def combine_a(p):
        for kind in (1, 0):
            for i in range(2):
                c_grad(p, i, kind).wait_recv()
                acc[p, 4 - 2 * core - 2 * i, kind] += rin[p, i, kind]
            ysend[p, 1, kind] = acc[p, 0, kind].astype(jnp.bfloat16)

            @pl.when(has_back)
            def _():
                y_grad(p, 1, kind).start()

    def combine_b(p):
        for kind in (1, 0):
            @pl.when(has_ahead)
            def _():
                y_grad(p, 1, kind).wait_recv()

            ysend[p, 0, kind] = (acc[p, 2, kind] + yin[p, 1, kind].astype(jnp.float32)).astype(jnp.bfloat16)

            @pl.when(has_back)
            def _():
                y_grad(p, 0, kind).start()

    def total_of(p, kind):
        @pl.when(has_ahead)
        def _():
            y_grad(p, 0, kind).wait_recv()

        return acc[p, 4, kind] + yin[p, 0, kind].astype(jnp.float32)

    def finish(p, kind, total):
        if kind == 0:
            total = total * score_scale
            total = total * small[0] - pltpu.roll(total, HEAD // 2, 1) * small[1]
        done[p, kind] = total.astype(jnp.bfloat16)

    def finish_swapped(p):
        for kind in (1, 0):
            finish(p, kind, total_of(p, kind))

            @pl.when(flip == 0)
            def _():
                own_out(p, kind).start()

            @pl.when(flip == 1)
            def _():
                x_out(p, kind).start()

    @pl.loop(0, PLACES)
    def _(p):
        for i in range(2):
            for kind in range(2):
                c_kv(p, i, kind).wait_recv()
        kt[...] = kv[p, :, 0].reshape(SPAN, HEAD).T

        @pl.when(p + 2 < PLACES)
        def _():
            stage_a(p + 2)

        weigh(p, p, 0)
        query_grads(p, 0)
        own_dq(p).start()

        @pl.when(p + 1 < PLACES)
        def _():
            stage_b(p + 1)

        @pl.when(p > 0)
        def _():
            combine_a(p - 1)

        @pl.when(p > 1)
        def _():
            combine_b(p - 2)

        x_q(p).wait_recv()
        x_g(p).wait_recv()
        rotate_queries(PLACES + p, 1)
        weigh(p, PLACES + p, 1)
        key_grads(p)
        query_grads(PLACES + p, 1)
        x_dq(p, mine).start()

        @pl.when(p + 1 < PLACES)
        def _():
            own_q(p + 1).wait()
            own_g(p + 1).wait()
            rotate_queries(p + 1, 0)

    combine_b(PLACES - 2)
    combine_a(PLACES - 1)
    finish_swapped(0)
    finish_swapped(1)
    combine_b(PLACES - 1)
    finish_swapped(2)
    finish_swapped(3)

    @pl.when(has_ahead)
    def _():
        for p in range(PLACES):
            for i in range(2):
                for kind in range(2):
                    y_kv(p, i, kind).wait_send()

    @pl.when(has_back)
    def _():
        for p in range(PLACES):
            for i in range(2):
                for kind in range(2):
                    y_grad(p, i, kind).wait_send()

    for p in range(PLACES):
        own_dq(p).wait()
        for i in range(2):
            for kind in range(2):
                c_kv(p, i, kind).wait_send()
                c_grad(p, i, kind).wait_send()
    for p in range(PLACES):
        x_q(p).wait_send()
        x_g(p).wait_send()
        x_dq(p, mine).wait_send()
        x_dq(p, theirs).wait_recv()

    @pl.when(flip == 0)
    def _():
        for p in range(PLACES):
            for i in range(2):
                own_out(p, i).wait()

    @pl.when(flip == 1)
    def _():
        for p in range(PLACES):
            for i in range(2):
                x_out(p, i).wait_send()
                x_out(p, i).wait_recv()


def settle(dq_ref, dkv_ref, dq_out, dk_out, dv_out, dq_here, dkv_here, in_sem, out_sem):
    pieces = []
    step = dq_ref.shape[0] // SETTLE
    for n in range(SETTLE):
        rows = pl.ds(n * step, step)
        pieces.append((dq_ref.at[rows], dq_here.at[rows], dq_out.at[rows]))
    pieces.append((dkv_ref.at[0], dkv_here.at[0], dk_out))
    pieces.append((dkv_ref.at[1], dkv_here.at[1], dv_out))
    arrivals = [pltpu.make_async_copy(a, b, in_sem.at[n]) for n, (a, b, _) in enumerate(pieces)]
    leaves = [pltpu.make_async_copy(b, c, out_sem.at[n]) for n, (_, b, c) in enumerate(pieces)]
    for copy in arrivals:
        copy.start()
    for arrival, leave in zip(arrivals, leaves):
        arrival.wait()
        leave.start()
    for leave in leaves:
        leave.wait()


def body(outer_count, inner_count, queries, keys, values, grad_out, positions):
    tokens, groups, width = queries.shape
    rows = tokens * groups
    half = OWN_HEADS * HEAD
    low, high = jnp.bfloat16, jnp.float32
    semaphores = pltpu.SemaphoreType.DMA
    swapped = OWN_HEADS
    pairs = (PLACES, 2)
    anywhere = pl.BlockSpec(memory_space=pl.ANY)
    off_chip = pl.BlockSpec(memory_space=pltpu.HBM)
    dq, dkv = pl.pallas_call(
        functools.partial(kernel, outer_count, inner_count, groups),
        out_shape=(
            jax.ShapeDtypeStruct((tokens, groups, width), low),
            jax.ShapeDtypeStruct((2, tokens, half), low),
        ),
        in_specs=[anywhere] * 2 + [off_chip] * 3,
        out_specs=(anywhere, off_chip),
        scratch_shapes=[
            pltpu.VMEM((2 * OWN_HEADS, tokens, groups, HEAD), low),
            pltpu.VMEM((2 * OWN_HEADS, tokens, groups, HEAD), low),
            pltpu.VMEM((2, rows, HEAD), low),
            pltpu.VMEM((2, rows, HEAD), low),
            pltpu.VMEM((PLACES, tokens, HEAD), low),
            pltpu.VMEM((PLACES, 5, 2, BLOCK, HEAD), low),
            pltpu.VMEM((1, tokens), jnp.int32),
            pltpu.VMEM((2, tokens, HEAD), high),
            pltpu.VMEM((2, rows, HEAD), high),
            pltpu.VMEM((2, SPAN - 64, CHUNK), high),
            pltpu.VMEM((SPAN, 2 * rows), low),
            pltpu.VMEM((SPAN, 2 * rows), low),
            pltpu.VMEM((HEAD, SPAN), low),
            pltpu.VMEM((PLACES, 5, 2, BLOCK, HEAD), high),
            pltpu.VMEM((PLACES, 2, 2, BLOCK, HEAD), high),
            pltpu.VMEM((PLACES, 2, 2, BLOCK, HEAD), low),
            pltpu.VMEM((PLACES, 2, 2, BLOCK, HEAD), low),
            pltpu.VMEM((2 * OWN_HEADS, tokens, groups, HEAD), low),
            pltpu.VMEM((PLACES, 2, BLOCK, HEAD), low),
            semaphores,
            semaphores((PLACES,)),
            semaphores((PLACES,)),
            semaphores((PLACES,)),
            semaphores((PLACES,)),
            semaphores((2, swapped)),
            semaphores((2, swapped)),
            semaphores((PLACES, 4)),
            semaphores((PLACES, 4)),
            semaphores((PLACES, 4)),
            semaphores((PLACES, 4)),
            semaphores((PLACES, 4)),
            semaphores((PLACES, 4)),
            semaphores((PLACES, 4)),
            semaphores((PLACES, 4)),
            semaphores((PLACES,)),
            semaphores((swapped,)),
            semaphores((swapped,)),
            semaphores(pairs),
            semaphores(pairs),
        ],
        compiler_params=pltpu.CompilerParams(collective_id=0, has_side_effects=True, vmem_limit_bytes=62 * 2**20),
    )(
        queries,
        grad_out,
        keys,
        values,
        positions.reshape(1, tokens),
    )
    return pl.pallas_call(
        settle,
        out_shape=(
            jax.ShapeDtypeStruct((tokens, groups, width), low),
            jax.ShapeDtypeStruct((tokens, half), low),
            jax.ShapeDtypeStruct((tokens, half), low),
        ),
        in_specs=[off_chip] * 2,
        out_specs=(off_chip,) * 3,
        scratch_shapes=[
            pltpu.VMEM((tokens, groups, width), low),
            pltpu.VMEM((2, tokens, half), low),
            semaphores((SETTLE + 2,)),
            semaphores((SETTLE + 2,)),
        ],
        compiler_params=pltpu.CompilerParams(vmem_limit_bytes=62 * 2**20),
    )(dq, dkv)


def solution(mesh):
    placed = (
        P(("outer", "inner"), "head", None),
        P(("outer", "inner"), None),
        P(("outer", "inner"), None),
        P(("outer", "inner"), "head", None),
        P(("outer", "inner")),
    )
    return jax.shard_map(
        functools.partial(body, mesh.shape["outer"], mesh.shape["inner"]),
        mesh=mesh,
        in_specs=placed,
        out_specs=(
            P(("outer", "inner"), "head", None),
            P(("outer", "inner"), "head"),
            P(("outer", "inner"), "head"),
        ),
        check_vma=False,
    )
```

```python
import functools
import math

import jax
import jax.numpy as jnp
import numpy as np
from jax import lax
from jax.experimental import pallas as pl
from jax.experimental.pallas import tpu as pltpu
from jax.sharding import PartitionSpec as P

HEAD = 128
BLOCK = 128
BEHIND = 512
SPAN = BLOCK + BEHIND
CHUNK = 256
OWN_HEADS = 4
PLACES = OWN_HEADS
SETTLE = 4

rope_theta = 500000.0
rope_factor = 128.0
initial_context = 8192.0
ramp_low = 1.0
ramp_high = 32.0
attention_factor = 1.0 + 0.1 * math.log(rope_factor)
score_scale = 1.0 / math.sqrt(HEAD)
exponent_scale = score_scale / math.log(2.0)
EXCLUDED = -1e30

MESH = pl.DeviceIdType.MESH
NT = (((1,), (1,)), ((), ()))


def yarn_frequencies():
    halves = HEAD // 2
    powers = rope_theta ** (-2.0 * np.arange(halves) / HEAD)
    turns = initial_context * powers / (2.0 * np.pi)
    blend = np.clip((turns - ramp_low) / (ramp_high - ramp_low), 0.0, 1.0)
    return np.asarray(powers * ((1.0 - blend) / rope_factor + blend), np.float32)


TURN_HIGH = 6.28125
TURN_MIDDLE = math.floor((2.0 * math.pi - TURN_HIGH) * 2.0**20) / 2.0**20
TURN_LOW = 2.0 * math.pi - TURN_HIGH - TURN_MIDDLE


def rope_tables(positions):
    lane = lax.broadcasted_iota(jnp.int32, (8, HEAD), 1)
    frequency = jnp.zeros((8, HEAD), jnp.float32)
    for index, value in enumerate(yarn_frequencies()):
        frequency = jnp.where(lax.rem(lane, HEAD // 2) == index, float(value), frequency)
    times = jnp.broadcast_to(positions.astype(jnp.float32), (BLOCK, HEAD)).T
    angles = times * frequency[0:1]
    turns = jnp.floor(angles * (0.5 / math.pi) + 0.5)
    rest = ((angles - turns * TURN_HIGH) - turns * TURN_MIDDLE) - turns * TURN_LOW
    signed = jnp.where(lane[0:1] < HEAD // 2, -attention_factor, attention_factor)
    return attention_factor * jnp.cos(rest), signed * jnp.sin(rest)


def dot(a, b):
    return jnp.dot(a, b, preferred_element_type=jnp.float32)


def kernel(
    outer_count, inner_count, groups,
    q_ref, g_ref, k_ref, v_ref, pos_ref,
    dq_ref, dkv_ref,
    qb, gb, qr, gr, kraw, kv, pos, small, tab, bias, ps, dss, kt, acc, rin, ysend, yin, dqs, done,
    pos_sem, k_sem, v_sem, q_sem, g_sem, xs_sem, xr_sem, ys_sem, yr_sem, cs_sem, cr_sem,
    gcs_sem, gcr_sem, gys_sem, gyr_sem, dql_sem, dqs_sem, dqr_sem, os_sem, or_sem,
):
    outer, inner, head = lax.axis_index("outer"), lax.axis_index("inner"), lax.axis_index("head")
    blocks = outer_count * inner_count
    half_outer = outer_count // 2
    block = outer * inner_count + inner
    core = lax.rem(inner, 2)
    later = lax.div(outer, half_outer)
    flip = 1 - later
    owner = lax.rem(head + flip, 2)
    first, last = block < 2, block >= blocks - 2
    has_back, has_ahead = block >= 2, block < blocks - 2

    def at(distance):
        target = lax.rem(block + distance + blocks, blocks)
        target_outer = lax.div(target, inner_count)
        target_head = lax.rem(owner + 1 - lax.div(target_outer, half_outer), 2)
        return (target_outer, lax.rem(target, inner_count), target_head)

    partner = (outer, inner, 1 - head)
    sibling = (outer, inner + 1 - 2 * core, head)
    ahead, back = at(2), at(-2)
    rows = BLOCK * groups
    mine = owner * (OWN_HEADS * HEAD)
    theirs = (1 - owner) * (OWN_HEADS * HEAD)

    def columns(start):
        return pl.ds(pl.multiple_of(start, HEAD), HEAD)

    def column_of(p):
        return mine + p * HEAD

    def local(src, dst, sem):
        return pltpu.make_async_copy(src, dst, sem)

    def remote(src, dst, send, recv, device):
        return pltpu.make_async_remote_copy(
            src_ref=src, dst_ref=dst, send_sem=send, recv_sem=recv, device_id=device, device_id_type=MESH
        )

    def own_k(p):
        return local(k_ref.at[:, columns(column_of(p))], kraw.at[p], k_sem.at[p])

    def own_v(p):
        return local(v_ref.at[:, columns(column_of(p))], kv.at[p, 4, 1], v_sem.at[p])

    def own_q(p):
        return local(q_ref.at[:, :, columns(column_of(p))], qb.at[p], q_sem.at[p])

    def own_g(p):
        return local(g_ref.at[:, :, columns(column_of(p))], gb.at[p], g_sem.at[p])

    def x_q(p):
        return remote(q_ref.at[:, :, columns(theirs + p * HEAD)], qb.at[PLACES + p], xs_sem.at[0, p], xr_sem.at[0, p], partner)

    def x_g(p):
        return remote(g_ref.at[:, :, columns(theirs + p * HEAD)], gb.at[PLACES + p], xs_sem.at[1, p], xr_sem.at[1, p], partner)

    def y_kv(p, i, kind):
        n = 2 * i + kind
        return remote(kv.at[p, 4 - 2 * i, kind], kv.at[p, 2 - 2 * i, kind], ys_sem.at[p], yr_sem.at[p, n], ahead)

    def c_kv(p, i, kind):
        n = 2 * i + kind
        src = kv.at[p, 4 - 2 * core - 2 * i, kind]
        return remote(src, kv.at[p, 3 - 2 * i, kind], cs_sem.at[p], cr_sem.at[p, n], sibling)

    def c_grad(p, i, kind):
        n = 2 * i + kind
        return remote(acc.at[p, 3 - 2 * i, kind], rin.at[p, i, kind], gcs_sem.at[p], gcr_sem.at[p, n], sibling)

    def y_grad(p, i, kind):
        n = 2 * i + kind
        return remote(ysend.at[p, i, kind], yin.at[p, i, kind], gys_sem.at[p], gyr_sem.at[p, n], back)

    def own_dq(p):
        return local(dqs.at[p], dq_ref.at[:, :, columns(column_of(p))], dql_sem.at[p])

    def x_dq(p, start):
        return remote(
            dqs.at[PLACES + p], dq_ref.at[:, :, columns(start + p * HEAD)], dqs_sem.at[p], dqr_sem.at[p], partner
        )

    def results(p):
        here = pl.ds(p * HEAD, HEAD)
        return ((done.at[p, 0], dkv_ref.at[0, :, here]), (done.at[p, 1], dkv_ref.at[1, :, here]))

    def own_out(p, i):
        src, dst = results(p)[i]
        return local(src, dst, os_sem.at[p, i])

    def x_out(p, i):
        src, dst = results(p)[i]
        return remote(src, dst, os_sem.at[p, i], or_sem.at[p, i], partner)

    times = local(pos_ref, pos, pos_sem)
    times.start()
    for p in range(PLACES):
        own_k(p).start()
        own_v(p).start()
    barrier = pltpu.get_barrier_semaphore()

    def greet(peer):
        pl.semaphore_signal(barrier, inc=1, device_id=peer, device_id_type=MESH)

    greet(partner)
    greet(sibling)

    @pl.when(has_ahead)
    def _():
        greet(ahead)

    @pl.when(has_back)
    def _():
        greet(back)

    times.wait()
    small[0], small[1] = rope_tables(pos[...])
    cosines, sines = small[0], small[1]
    for p in range(PLACES):
        own_k(p).wait()
        raw = kraw[p].astype(jnp.float32)
        kv[p, 4, 0] = (raw * cosines + pltpu.roll(raw, HEAD // 2, 1) * sines).astype(jnp.bfloat16)
    for p in range(PLACES):
        own_v(p).wait()
    @pl.when(has_ahead & has_back)
    def _():
        pl.semaphore_wait(barrier, 4)

    @pl.when(first | last)
    def _():
        pl.semaphore_wait(barrier, 3)

    @pl.when(first)
    def _():
        for p in range(PLACES):
            kv[p, 0] = jnp.zeros((2, BLOCK, HEAD), jnp.bfloat16)
            kv[p, 2] = jnp.zeros((2, BLOCK, HEAD), jnp.bfloat16)

    @pl.when(last)
    def _():
        yin[...] = jnp.zeros(yin.shape, jnp.bfloat16)


    def send_own(p):
        @pl.when(has_ahead)
        def _():
            for kind in range(2):
                y_kv(p, 0, kind).start()

    send_own(0)
    send_own(1)
    for p in range(PLACES):
        x_q(p).start()
        x_g(p).start()
    for p in range(PLACES):
        own_q(p).start()
        own_g(p).start()

    def stage_a(p):
        for kind in range(2):
            @pl.when(has_back)
            def _():
                y_kv(p, 0, kind).wait_recv()

            @pl.when(has_ahead)
            def _():
                y_kv(p, 1, kind).start()

            c_kv(p, 0, kind).start()

        @pl.when(p + 2 < PLACES)
        def _():
            send_own(p + 2)

    def stage_b(p):
        for kind in range(2):
            @pl.when(has_back)
            def _():
                y_kv(p, 1, kind).wait_recv()

            c_kv(p, 1, kind).start()

    low = lax.broadcasted_iota(jnp.int32, (8, HEAD), 0) < 4
    for table in (0, 1):
        for pair in range(BLOCK // 2):
            first = jnp.broadcast_to(small[table, 2 * pair:2 * pair + 1, :], (8, HEAD))
            second = jnp.broadcast_to(small[table, 2 * pair + 1:2 * pair + 2, :], (8, HEAD))
            tab[table, 8 * pair:8 * pair + 8, :] = jnp.where(low, first, second)

    stage_a(0)
    for part in (0, 1):
        row = lax.broadcasted_iota(jnp.int32, (SPAN - 64, CHUNK), 0)
        token = lax.broadcasted_iota(jnp.int32, (SPAN - 64, CHUNK), 1) // groups
        allowed = (row > token) & (row <= token + BEHIND) & (block * BLOCK - BEHIND + 64 * part + row >= 0)
        bias[part] = jnp.where(allowed, 0.0, EXCLUDED).astype(jnp.float32)
    for low_precision in (ps, dss):
        for side in (0, 2 * CHUNK):
            low_precision[SPAN - 64:, side:side + CHUNK] = jnp.zeros((64, CHUNK), jnp.bfloat16)
            low_precision[:64, side + CHUNK:side + 2 * CHUNK] = jnp.zeros((64, CHUNK), jnp.bfloat16)
    stage_a(1)

    def rotate_queries(n, side):
        raw = qb[n].reshape(rows, HEAD).astype(jnp.float32)
        gr[side] = gb[n].reshape(rows, HEAD)
        qr[side] = (raw * tab[0] + pltpu.roll(raw, HEAD // 2, 1) * tab[1]).astype(jnp.bfloat16)

    own_q(0).wait()
    own_g(0).wait()
    rotate_queries(0, 0)
    stage_b(0)

    def weigh(p, n, side):
        keys = kv[p, :, 0].reshape(SPAN, HEAD)
        values = kv[p, :, 1].reshape(SPAN, HEAD)
        for part in (0, 1):
            here = slice(CHUNK * part, CHUNK * part + CHUNK)
            there = slice(rows * side + CHUNK * part, rows * side + CHUNK * part + CHUNK)
            seen = slice(64 * part, 64 * part + SPAN - 64)
            scores = lax.dot_general(keys[seen], qr[side, here], NT, preferred_element_type=jnp.float32) + bias[part]
            top = jnp.max(scores, 0, keepdims=True)
            raised = jnp.exp2((scores - top) * exponent_scale)
            weights = raised * (1.0 / jnp.sum(raised, 0, keepdims=True))
            grads = lax.dot_general(values[seen], gr[side, here], NT, preferred_element_type=jnp.float32)
            delta = jnp.sum(weights * grads, 0, keepdims=True)
            ps[seen, there] = weights.astype(jnp.bfloat16)
            dss[seen, there] = (weights * (grads - delta)).astype(jnp.bfloat16)

    def query_grads(n, side):
        query_part = dot(kt[...], dss[:, rows * side:rows * side + rows]).T
        query_part = query_part * score_scale
        rotated = query_part * tab[0] - pltpu.roll(query_part, HEAD // 2, 1) * tab[1]
        dqs[n] = rotated.astype(jnp.bfloat16).reshape(BLOCK, groups, HEAD)

    def key_grads(p):
        for kind, weights, vectors in ((1, ps, gr), (0, dss, qr)):
            acc[p, :, kind] = dot(weights[...], vectors[...].reshape(2 * rows, HEAD)).reshape(5, BLOCK, HEAD)
            for i in range(2):
                c_grad(p, i, kind).start()

    def combine_a(p):
        for kind in (1, 0):
            for i in range(2):
                c_grad(p, i, kind).wait_recv()
                acc[p, 4 - 2 * core - 2 * i, kind] += rin[p, i, kind]
            ysend[p, 1, kind] = acc[p, 0, kind].astype(jnp.bfloat16)

            @pl.when(has_back)
            def _():
                y_grad(p, 1, kind).start()

    def combine_b(p):
        for kind in (1, 0):
            @pl.when(has_ahead)
            def _():
                y_grad(p, 1, kind).wait_recv()

            ysend[p, 0, kind] = (acc[p, 2, kind] + yin[p, 1, kind].astype(jnp.float32)).astype(jnp.bfloat16)

            @pl.when(has_back)
            def _():
                y_grad(p, 0, kind).start()

    def total_of(p, kind):
        @pl.when(has_ahead)
        def _():
            y_grad(p, 0, kind).wait_recv()

        return acc[p, 4, kind] + yin[p, 0, kind].astype(jnp.float32)

    def finish(p, kind, total):
        if kind == 0:
            total = total * score_scale
            total = total * small[0] - pltpu.roll(total, HEAD // 2, 1) * small[1]
        done[p, kind] = total.astype(jnp.bfloat16)

    def finish_swapped(p):
        for kind in (1, 0):
            finish(p, kind, total_of(p, kind))

            @pl.when(flip == 0)
            def _():
                own_out(p, kind).start()

            @pl.when(flip == 1)
            def _():
                x_out(p, kind).start()

    @pl.loop(0, PLACES)
    def _(p):
        for i in range(2):
            for kind in range(2):
                c_kv(p, i, kind).wait_recv()
        kt[...] = kv[p, :, 0].reshape(SPAN, HEAD).T

        @pl.when(p + 2 < PLACES)
        def _():
            stage_a(p + 2)

        weigh(p, p, 0)
        query_grads(p, 0)
        own_dq(p).start()

        @pl.when(p + 1 < PLACES)
        def _():
            stage_b(p + 1)

        @pl.when(p > 0)
        def _():
            combine_a(p - 1)

        @pl.when(p > 1)
        def _():
            combine_b(p - 2)

        x_q(p).wait_recv()
        x_g(p).wait_recv()
        rotate_queries(PLACES + p, 1)
        weigh(p, PLACES + p, 1)
        key_grads(p)
        query_grads(PLACES + p, 1)
        x_dq(p, mine).start()

        @pl.when(p + 1 < PLACES)
        def _():
            own_q(p + 1).wait()
            own_g(p + 1).wait()
            rotate_queries(p + 1, 0)

    combine_b(PLACES - 2)
    combine_a(PLACES - 1)
    finish_swapped(0)
    finish_swapped(1)
    combine_b(PLACES - 1)
    finish_swapped(2)
    finish_swapped(3)

    def sent(ref, p, sem, recv, device):
        whole = ref.at[p, pl.ds(0, 2)]
        remote(whole, whole, sem.at[p], recv.at[p, 0], device).wait_send()

    @pl.when(has_ahead)
    def _():
        for p in range(PLACES):
            sent(kv, p, ys_sem, yr_sem, ahead)

    @pl.when(has_back)
    def _():
        for p in range(PLACES):
            sent(ysend, p, gys_sem, gyr_sem, back)

    for p in range(PLACES):
        sent(kv, p, cs_sem, cr_sem, sibling)
        sent(acc, p, gcs_sem, gcr_sem, sibling)
    for p in range(PLACES):
        own_dq(p).wait()
    for p in range(PLACES):
        x_q(p).wait_send()
        x_g(p).wait_send()
        x_dq(p, mine).wait_send()
        x_dq(p, theirs).wait_recv()

    @pl.when(flip == 0)
    def _():
        for p in range(PLACES):
            for i in range(2):
                own_out(p, i).wait()

    @pl.when(flip == 1)
    def _():
        for p in range(PLACES):
            for i in range(2):
                x_out(p, i).wait_send()
                x_out(p, i).wait_recv()


def settle(dq_ref, dkv_ref, dq_out, dk_out, dv_out, dq_here, dkv_here, in_sem, out_sem):
    pieces = []
    step = dq_ref.shape[0] // SETTLE
    for n in range(SETTLE):
        rows = pl.ds(n * step, step)
        pieces.append((dq_ref.at[rows], dq_here.at[rows], dq_out.at[rows]))
    pieces.append((dkv_ref.at[0], dkv_here.at[0], dk_out))
    pieces.append((dkv_ref.at[1], dkv_here.at[1], dv_out))
    arrivals = [pltpu.make_async_copy(a, b, in_sem.at[n]) for n, (a, b, _) in enumerate(pieces)]
    leaves = [pltpu.make_async_copy(b, c, out_sem.at[n]) for n, (_, b, c) in enumerate(pieces)]
    for copy in arrivals:
        copy.start()
    for arrival, leave in zip(arrivals, leaves):
        arrival.wait()
        leave.start()
    for leave in leaves:
        leave.wait()


def body(outer_count, inner_count, queries, keys, values, grad_out, positions):
    tokens, groups, width = queries.shape
    rows = tokens * groups
    half = OWN_HEADS * HEAD
    low, high = jnp.bfloat16, jnp.float32
    semaphores = pltpu.SemaphoreType.DMA
    swapped = OWN_HEADS
    pairs = (PLACES, 2)
    anywhere = pl.BlockSpec(memory_space=pl.ANY)
    off_chip = pl.BlockSpec(memory_space=pltpu.HBM)
    dq, dkv = pl.pallas_call(
        functools.partial(kernel, outer_count, inner_count, groups),
        out_shape=(
            jax.ShapeDtypeStruct((tokens, groups, width), low),
            jax.ShapeDtypeStruct((2, tokens, half), low),
        ),
        in_specs=[anywhere] * 2 + [off_chip] * 3,
        out_specs=(anywhere, off_chip),
        scratch_shapes=[
            pltpu.VMEM((2 * OWN_HEADS, tokens, groups, HEAD), low),
            pltpu.VMEM((2 * OWN_HEADS, tokens, groups, HEAD), low),
            pltpu.VMEM((2, rows, HEAD), low),
            pltpu.VMEM((2, rows, HEAD), low),
            pltpu.VMEM((PLACES, tokens, HEAD), low),
            pltpu.VMEM((PLACES, 5, 2, BLOCK, HEAD), low),
            pltpu.VMEM((1, tokens), jnp.int32),
            pltpu.VMEM((2, tokens, HEAD), high),
            pltpu.VMEM((2, rows, HEAD), high),
            pltpu.VMEM((2, SPAN - 64, CHUNK), high),
            pltpu.VMEM((SPAN, 2 * rows), low),
            pltpu.VMEM((SPAN, 2 * rows), low),
            pltpu.VMEM((HEAD, SPAN), low),
            pltpu.VMEM((PLACES, 5, 2, BLOCK, HEAD), high),
            pltpu.VMEM((PLACES, 2, 2, BLOCK, HEAD), high),
            pltpu.VMEM((PLACES, 2, 2, BLOCK, HEAD), low),
            pltpu.VMEM((PLACES, 2, 2, BLOCK, HEAD), low),
            pltpu.VMEM((2 * OWN_HEADS, tokens, groups, HEAD), low),
            pltpu.VMEM((PLACES, 2, BLOCK, HEAD), low),
            semaphores,
            semaphores((PLACES,)),
            semaphores((PLACES,)),
            semaphores((PLACES,)),
            semaphores((PLACES,)),
            semaphores((2, swapped)),
            semaphores((2, swapped)),
            semaphores((PLACES,)),
            semaphores((PLACES, 4)),
            semaphores((PLACES,)),
            semaphores((PLACES, 4)),
            semaphores((PLACES,)),
            semaphores((PLACES, 4)),
            semaphores((PLACES,)),
            semaphores((PLACES, 4)),
            semaphores((PLACES,)),
            semaphores((swapped,)),
            semaphores((swapped,)),
            semaphores(pairs),
            semaphores(pairs),
        ],
        compiler_params=pltpu.CompilerParams(collective_id=0, has_side_effects=True, vmem_limit_bytes=62 * 2**20),
    )(
        queries,
        grad_out,
        keys,
        values,
        positions.reshape(1, tokens),
    )
    return pl.pallas_call(
        settle,
        out_shape=(
            jax.ShapeDtypeStruct((tokens, groups, width), low),
            jax.ShapeDtypeStruct((tokens, half), low),
            jax.ShapeDtypeStruct((tokens, half), low),
        ),
        in_specs=[off_chip] * 2,
        out_specs=(off_chip,) * 3,
        scratch_shapes=[
            pltpu.VMEM((tokens, groups, width), low),
            pltpu.VMEM((2, tokens, half), low),
            semaphores((SETTLE + 2,)),
            semaphores((SETTLE + 2,)),
        ],
        compiler_params=pltpu.CompilerParams(vmem_limit_bytes=62 * 2**20),
    )(dq, dkv)


def solution(mesh):
    placed = (
        P(("outer", "inner"), "head", None),
        P(("outer", "inner"), None),
        P(("outer", "inner"), None),
        P(("outer", "inner"), "head", None),
        P(("outer", "inner")),
    )
    return jax.shard_map(
        functools.partial(body, mesh.shape["outer"], mesh.shape["inner"]),
        mesh=mesh,
        in_specs=placed,
        out_specs=(
            P(("outer", "inner"), "head", None),
            P(("outer", "inner"), "head"),
            P(("outer", "inner"), "head"),
        ),
        check_vma=False,
    )
```
